256 devices in a mesh: row: 16 (over z, core), col: 4 (over x), seed: 4 (over y).
Axes of the slice: x: 4, y: 4, z: 8, core: 2. Of those that a mesh axis runs over, the one named last changes fastest.
Arguments:
- tiles: bfloat16 [16, 4, 384, 128, 128], P('row', 'col'), may hold values from -0.0390625 to 0.0390625
- tile_out: int32 [16, 4, 384], P('row', 'col'), may hold values from 0 to 15, as said below
- tile_in: int32 [16, 4, 384], P('row', 'col'), may hold values from 0 to 3
- tile_count: int32 [16, 4], P('row', 'col'), may hold values from 1 to 384, as said below
- out_degree: int32 [8192], P(('row', 'col')), may hold values from 1 to 8
- seed_ids: int32 [512, 16], P('seed'), may hold values from 0 to 8191
- prior: float32 [512, 8192], P('seed', ('row', 'col')), may hold values from -6 to 6
Outputs:
- risk: float32 [512, 8192], P('seed', ('row', 'col'))
The draws below stay inside these ranges and needn't reach their ends.
Inputs may be any that keep to these rules, and one draw needn't show every extreme that they name: `tile_count`: occupied slots of a device come first; some device has all 384 occupied in every draw. `tile_out`: on every device the output blocks named by the occupied slots never fall from one slot to the next; several occupied slots of one device may name the same output block, and the same pair of blocks.
All inputs are finite; a program needn't handle non-finite values.
Results may differ from the reference program's by a relative error of at most 0.0041.
Values may be sent and summed in bfloat16 or wider, within the bound.
A program may use at most 64 MiB of HBM per device.

```python
import jax
import jax.numpy as jnp
from jax import lax

VERTEX_DEV = 128
TILE_SLOTS = 384
TILE_EDGE = 128
SEED_COUNT = 16
ITERATIONS = 2
SEED_SETS = 512
VERTICES = 8192
OUT_BLOCKS = 16
IN_BLOCKS = 4
N_ROW = 16
N_COL = 4


def count_table(key):
    first_key, second_key, third_key = jax.random.split(jax.random.fold_in(key, 7), 3)
    device_total = N_ROW * N_COL
    divisor = 1 + jax.random.randint(first_key, (device_total,), 0, 4)
    lowered = jax.random.randint(second_key, (device_total,), 1, 32)
    counts = jnp.maximum(TILE_SLOTS // divisor - lowered, 1)
    chosen = jax.random.randint(third_key, (), 0, device_total)
    counts = counts.at[chosen].set(TILE_SLOTS)
    return counts.astype(jnp.int32)


def draw_tile_count(key, part):
    return count_table(key).reshape(N_ROW, N_COL)


def draw_tile_out(key, part):
    counts = count_table(key).reshape(N_ROW * N_COL, 1)
    raw_blocks = jax.random.randint(jax.random.fold_in(key, 11), (N_ROW * N_COL, TILE_SLOTS), 0, OUT_BLOCKS)
    slot_order = jnp.arange(TILE_SLOTS, dtype=jnp.int32)[None, :]
    keyed = jnp.where(slot_order < counts, raw_blocks, raw_blocks + OUT_BLOCKS)
    ordered = jnp.sort(keyed, axis=1)
    ordered = jnp.where(ordered >= OUT_BLOCKS, ordered - OUT_BLOCKS, ordered)
    return ordered.reshape(N_ROW, N_COL, TILE_SLOTS).astype(jnp.int32)


def touch_ends(drawn, stream_key, least, largest):
    longest = drawn.shape.index(max(drawn.shape))
    spots = []
    for shift in (0, 1):
        where = [jax.random.randint(jax.random.fold_in(stream_key, axis), (), 0, length) for axis, length in enumerate(drawn.shape)]
        where[longest] = (where[longest] + shift) % drawn.shape[longest]
        spots.append(tuple(where))
    return drawn.at[spots[0]].set(least).at[spots[1]].set(largest)


def block_scale(key, dims, cuts, smallest, high):
    def one(dim, shards_of):
        draws = jax.random.uniform(jax.random.fold_in(jax.random.fold_in(key, 6), dim), (shards_of,), jnp.float32, smallest / len(cuts), high / len(cuts))
        return jnp.repeat(jnp.exp(draws), dims[dim] // shards_of).reshape((-1,) + (1,) * (len(dims) - dim - 1))

    factor_of = one(*cuts[0])
    for cut in cuts[1:]:
        factor_of = factor_of * one(*cut)
    return factor_of


def normal_values(rng, extent, spread, reach, cuts=(), held_as=jnp.bfloat16):
    values = spread * jax.random.normal(rng, extent, jnp.float32)
    if cuts:
        values = values * block_scale(rng, extent, cuts, -0.22, 0.18)
    return jnp.clip(values, -reach, reach).astype(held_as)


def setup_inputs(seed: int = 0) -> dict:
    seeds = jax.random.split(jax.random.key(seed), 8)
    return {
        "tiles": normal_values(seeds[0], (N_ROW, N_COL, TILE_SLOTS, TILE_EDGE, TILE_EDGE), (TILE_EDGE * TILE_EDGE * TILE_SLOTS // (2 * VERTEX_DEV)) ** -0.5, 0.0390625, ((0, 16), (1, 4))),
        "tile_out": draw_tile_out(jax.random.fold_in(seeds[7], 71), 0),
        "tile_in": touch_ends(jax.random.randint(seeds[2], (N_ROW, N_COL, TILE_SLOTS), 0, IN_BLOCKS), jax.random.fold_in(seeds[2], 1), 0, IN_BLOCKS - 1).astype(jnp.int32),
        "tile_count": draw_tile_count(jax.random.fold_in(seeds[7], 71), 0),
        "out_degree": touch_ends(jax.random.randint(seeds[4], (VERTICES,), 1, 9), jax.random.fold_in(seeds[4], 1), 1, 8).astype(jnp.int32),
        "seed_ids": touch_ends(jax.random.randint(seeds[5], (SEED_SETS, SEED_COUNT), 0, VERTICES), jax.random.fold_in(seeds[5], 1), 0, VERTICES - 1).astype(jnp.int32),
        "prior": normal_values(seeds[6], (SEED_SETS, VERTICES), 1.0, 6.0, ((0, 4), (1, 64)), jnp.float32),
    }


damping = 0.85


def reference(tiles, tile_out, tile_in, tile_count, out_degree, seed_ids, prior):
    set_rows = jnp.broadcast_to(jnp.arange(SEED_SETS, dtype=jnp.int32)[:, None], seed_ids.shape)
    restart = jnp.zeros((SEED_SETS, VERTICES), jnp.float32).at[set_rows, seed_ids].add(1.0)
    degree = out_degree.astype(jnp.float32)
    slot_index = jnp.arange(TILE_SLOTS, dtype=jnp.int32)
    row_order = jnp.arange(N_ROW, dtype=jnp.int32)
    risk_now = prior
    for round_index in range(ITERATIONS):
        scaled = (risk_now / degree[None, :]).astype(jnp.bfloat16)
        inputs = scaled.reshape(SEED_SETS, N_ROW, IN_BLOCKS, TILE_EDGE)
        columns = []
        for col_index in range(N_COL):
            def add_device(panel_sum, row_index):
                block_in = inputs[:, row_index]
                gathered = jnp.take(block_in, tile_in[row_index, col_index], axis=1).astype(jnp.float32)
                weights = tiles[row_index, col_index].astype(jnp.float32)
                product = jnp.einsum("stk,tkj->stj", gathered, weights)
                valid_mask = (slot_index < tile_count[row_index, col_index]).astype(jnp.float32)
                product = product * valid_mask[None, :, None]
                return panel_sum.at[:, tile_out[row_index, col_index], :].add(product), None

            zero_panel = jnp.zeros((SEED_SETS, OUT_BLOCKS, TILE_EDGE), jnp.float32)
            panel_sum, _ = lax.scan(add_device, zero_panel, row_order)
            columns.append(panel_sum.reshape(SEED_SETS, N_ROW, VERTEX_DEV))
        incoming = jnp.stack(columns, axis=2).reshape(SEED_SETS, VERTICES)
        risk_now = (1.0 - damping) * restart + damping * incoming
    return risk_now
```

```python
import functools
import math

import jax
import jax.numpy as jnp
from jax import lax
from jax.experimental import pallas as pl
from jax.experimental.pallas import tpu as pltpu
from jax.sharding import PartitionSpec as P

ITERATIONS = 2
PARTS = 4
damping = 0.85
MESH = pl.DeviceIdType.MESH


def ring_order(ring):
    return sorted(range(ring), key=lambda d: -min(d, ring - d))


def kernel(
    rows, cols, chunks,
    count, outs, ins, tiles, degree, seeds, prior, risk_out,
    buf, sum0, sum1, sum2, sum3, heads, w, xs, own, psend, precv, zsend, zrecv,
    tsem, xs_send, xs_recv, ps_send, ps_recv, zs_send, zs_recv,
):
    sums = (sum0, sum1, sum2, sum3)
    slots, edge, _ = buf.shape
    group = slots // chunks
    part = edge // PARTS
    ring = rows // 2
    row = lax.axis_index("row")
    col = lax.axis_index("col")
    core = lax.rem(row, 2)
    chip = row // 2
    partner = row + 1 - 2 * core
    depth = cols * edge
    order = ring_order(ring)
    none = slots

    def tile_copy(g):
        at = pl.ds(g * group, group)
        return pltpu.make_async_copy(tiles.at[at], buf.at[at], tsem.at[g])

    barrier = pltpu.get_barrier_semaphore()
    for d in range(1, cols):
        pl.semaphore_signal(barrier, inc=1, device_id={"col": lax.rem(col + d, cols)}, device_id_type=MESH)
    pl.semaphore_signal(barrier, inc=1, device_id={"row": partner}, device_id_type=MESH)
    for d in range(1, ring):
        peer = lax.rem(chip + d, ring) * 2 + core
        pl.semaphore_signal(barrier, inc=1, device_id={"row": peer}, device_id_type=MESH)
    for g in range(chunks):
        tile_copy(g).start()

    degrees = degree[...].astype(jnp.float32)

    def gather(step, risk):
        xs[step, col] = (risk / degrees).astype(jnp.bfloat16)
        copies = []
        for d in range(1, cols):
            copy = pltpu.make_async_remote_copy(
                src_ref=xs.at[step, col],
                dst_ref=xs.at[step, col],
                send_sem=xs_send.at[step, d - 1],
                recv_sem=xs_recv.at[step, d - 1],
                device_id={"col": lax.rem(col + d, cols)},
                device_id_type=MESH,
            )
            copies.append(copy)
        return copies

    first_copies = gather(0, prior[...])
    pl.semaphore_wait(barrier, cols - 1 + 1 + ring - 1)
    for copy in first_copies:
        copy.start()

    for q in range(PARTS):
        sums[q][none] = jnp.zeros((part, edge), jnp.float32)

    def add_tile(s, carry):
        last_out, last_in = carry[0], carry[1:]
        o = outs[s]
        i = ins[s]
        same = o == last_out
        last_in = [jnp.where(same, h, none) for h in last_in]
        prev = last_in[0]
        for k in range(1, cols):
            prev = jnp.where(i == k, last_in[k], prev)
        for q in range(PARTS):
            tile = buf[s, q * part:(q + 1) * part, :].astype(jnp.float32)
            sums[q][s] = sums[q][prev] + tile
        last_in = [jnp.where(i == k, s, last_in[k]) for k in range(cols)]
        for k in range(0, cols, 2):
            heads[k // 2, s] = last_in[k] + last_in[k + 1] * 65536
        return (o, *last_in)

    carry = (jnp.int32(-1),) + (jnp.int32(none),) * cols
    for g in range(chunks):
        tile_copy(g).wait()
        carry = lax.fori_loop(g * group, (g + 1) * group, add_tile, carry, unroll=4)

    used = count[0]
    steps = [1 << b for b in reversed(range(slots.bit_length()))]

    def last_slots(o):
        end = jnp.int32(0)
        for step in steps:
            mid = end + step
            inside = mid <= used
            fits = outs[jnp.minimum(mid, slots) - 1] <= o
            end = jnp.where(inside & fits, mid, end)
        at = jnp.maximum(end - 1, 0)
        hit = (end > 0) & (outs[at] == o)
        found = []
        for k in range(0, cols, 2):
            pair = heads[k // 2, at]
            found.append(jnp.where(hit, pair % 65536, none))
            found.append(jnp.where(hit, pair // 65536, none))
        return found

    def build(n, target):
        for half in range(2):
            places = last_slots(target * 2 + half)
            for k in range(cols):
                for q in range(PARTS):
                    value = sums[q][places[k]]
                    high = value.astype(jnp.bfloat16)
                    low = (value - high.astype(jnp.float32)).astype(jnp.bfloat16)
                    at = k * edge + q * part
                    w[n, at:at + part, half * edge:(half + 1) * edge] = high
                    w[n, depth + at:depth + at + part, half * edge:(half + 1) * edge] = low

    start = (row * cols + col) * edge
    restart = None
    incoming = None
    for step in range(ITERATIONS):
        copies = first_copies if step == 0 else gather(step, risk)
        if step > 0:
            for copy in copies:
                copy.start()
        for copy in copies:
            copy.wait()
        parts = [xs[step, k] for k in range(cols)]
        x = jnp.concatenate(parts + parts, axis=1)
        partner_copies = []
        for n, d in enumerate(order):
            target = lax.rem(chip + d, ring)
            if step == 0:
                build(n, target)
            both = jnp.dot(x, w[n], preferred_element_type=jnp.float32)
            left, right = both[:, :edge], both[:, edge:]
            psend[step, n] = jnp.where(core == 0, right, left).astype(jnp.bfloat16)
            copy = pltpu.make_async_remote_copy(
                src_ref=psend.at[step, n],
                dst_ref=precv.at[step, n],
                send_sem=ps_send.at[step, n],
                recv_sem=ps_recv.at[step, n],
                device_id={"row": partner},
                device_id_type=MESH,
            )
            copy.start()
            partner_copies.append(copy)
            own[n] = jnp.where(core == 0, left, right)
        chip_copies = []
        for n, d in enumerate(order):
            partner_copies[n].wait()
            total = own[n] + precv[step, n].astype(jnp.float32)
            if d == 0:
                incoming = total
            else:
                zsend[step, n] = total.astype(jnp.bfloat16)
                copy = pltpu.make_async_remote_copy(
                    src_ref=zsend.at[step, n],
                    dst_ref=zrecv.at[step, n],
                    send_sem=zs_send.at[step, n],
                    recv_sem=zs_recv.at[step, n],
                    device_id={"row": lax.rem(chip + d, ring) * 2 + core},
                    device_id_type=MESH,
                )
                copy.start()
                chip_copies.append((n, copy))
        if step == 0:
            local_ids = seeds[...] - start
            places = lax.broadcasted_iota(jnp.int32, (local_ids.shape[0], edge), 1)
            restart = jnp.zeros(places.shape, jnp.float32)
            for j in range(local_ids.shape[1]):
                restart += (local_ids[:, j:j + 1] == places).astype(jnp.float32)
        for n, copy in reversed(chip_copies):
            copy.wait()
            incoming += zrecv[step, n].astype(jnp.float32)
        risk = (1.0 - damping) * restart + damping * incoming
    risk_out[...] = risk


def local(tiles, tile_out, tile_in, tile_count, out_degree, seed_ids, prior):
    rows, cols = lax.axis_size("row"), lax.axis_size("col")
    slots, edge = tiles.shape[2], tiles.shape[4]
    sets = prior.shape[0]
    ring = rows // 2
    chunks = math.gcd(slots, 8)
    vmem = pl.BlockSpec(memory_space=pltpu.VMEM)
    smem = pl.BlockSpec(memory_space=pltpu.SMEM)
    hbm = pl.BlockSpec(memory_space=pl.ANY)
    block = (sets, edge)
    dma = pltpu.SemaphoreType.DMA
    return pl.pallas_call(
        functools.partial(kernel, rows, cols, chunks),
        out_shape=jax.ShapeDtypeStruct(block, jnp.float32),
        in_specs=[smem, smem, smem, hbm, vmem, vmem, vmem],
        out_specs=vmem,
        scratch_shapes=[
            pltpu.VMEM((slots, edge, edge), jnp.bfloat16),
            *[pltpu.VMEM((slots + 1, edge // PARTS, edge), jnp.float32) for _ in range(PARTS)],
            pltpu.SMEM((cols // 2, slots), jnp.int32),
            pltpu.VMEM((ring, 2 * cols * edge, 2 * edge), jnp.bfloat16),
            pltpu.VMEM((ITERATIONS, cols, *block), jnp.bfloat16),
            pltpu.VMEM((ring, *block), jnp.float32),
            pltpu.VMEM((ITERATIONS, ring, *block), jnp.bfloat16),
            pltpu.VMEM((ITERATIONS, ring, *block), jnp.bfloat16),
            pltpu.VMEM((ITERATIONS, ring, *block), jnp.bfloat16),
            pltpu.VMEM((ITERATIONS, ring, *block), jnp.bfloat16),
            dma((chunks,)),
            dma((ITERATIONS, cols)),
            dma((ITERATIONS, cols)),
            dma((ITERATIONS, ring)),
            dma((ITERATIONS, ring)),
            dma((ITERATIONS, ring)),
            dma((ITERATIONS, ring)),
        ],
        compiler_params=pltpu.CompilerParams(
            collective_id=0, has_side_effects=True, vmem_limit_bytes=60 * 1024 * 1024
        ),
    )(
        tile_count.reshape(1),
        tile_out.reshape(slots),
        tile_in.reshape(slots),
        tiles.reshape(slots, edge, edge),
        out_degree.reshape(1, edge),
        seed_ids,
        prior,
    )


def solution(mesh):
    placed = (
        P("row", "col", None, None, None),
        P("row", "col", None),
        P("row", "col", None),
        P("row", "col"),
        P(("row", "col")),
        P("seed", None),
        P("seed", ("row", "col")),
    )
    return jax.shard_map(
        local, mesh=mesh, in_specs=placed, out_specs=P("seed", ("row", "col")), check_vma=False
    )
```

```python
import functools
import math

import jax
import jax.numpy as jnp
from jax import lax
from jax.experimental import pallas as pl
from jax.experimental.pallas import tpu as pltpu
from jax.sharding import PartitionSpec as P

ITERATIONS = 2
PARTS = 4
CHUNKS = 16
FLIGHT = 4
HALVES = 2
X_CHUNK = 2
Z_CHUNK = 12
LAG_FIRST = 3
LAG_LAST = 5
damping = 0.85
MESH = pl.DeviceIdType.MESH


def ring_order(ring):
    return sorted(range(ring), key=lambda d: -min(d, ring - d))


def kernel(
    rows, cols, chunks,
    count, outs_in, ins_in, tiles, degree_in, seeds_in, prior_in, risk_out,
    outs, ins, degree, seeds, prior, buf, sum0, sum1, sum2, sum3, heads,
    w, xs, own, psend, precv, zsend, zrecv,
    isem, tsem, xs_send, xs_recv, ps_send, ps_recv, zs_send, zs_recv, x_ready, z_ready,
):
    sums = (sum0, sum1, sum2, sum3)
    slots, edge, _ = buf.shape
    sets = prior.shape[0]
    size = sets // HALVES
    group = slots // chunks
    part = edge // PARTS
    ring = rows // 2
    row = lax.axis_index("row")
    col = lax.axis_index("col")
    core = lax.rem(row, 2)
    chip = row // 2
    partner = row + 1 - 2 * core
    depth = cols * edge
    order = ring_order(ring)
    none = slots
    sent = []

    def tile_copy(g):
        at = pl.ds(g * group, group)
        return pltpu.make_async_copy(tiles.at[at], buf.at[at], tsem.at[g])

    def send(source, target, send_sem, recv_sem, device):
        copy = pltpu.make_async_remote_copy(
            src_ref=source, dst_ref=target, send_sem=send_sem, recv_sem=recv_sem,
            device_id=device, device_id_type=MESH,
        )
        copy.start()
        sent.append(copy)
        return copy

    small = [
        pltpu.make_async_copy(source, place, isem.at[n])
        for n, (source, place) in enumerate((
            (degree_in, degree), (prior_in, prior), (outs_in, outs), (ins_in, ins), (seeds_in, seeds),
        ))
    ]
    for copy in small:
        copy.start()
    for g in range(FLIGHT):
        tile_copy(g).start()

    barrier = pltpu.get_barrier_semaphore()
    for d in range(1, cols):
        pl.semaphore_signal(
            barrier, inc=1, device_id={"row": chip * 2, "col": lax.rem(col + d, cols)}, device_id_type=MESH
        )
    pl.semaphore_signal(barrier, inc=1, device_id={"row": partner}, device_id_type=MESH)
    for d in range(1, ring):
        peer = lax.rem(chip + d, ring) * 2 + 1
        pl.semaphore_signal(barrier, inc=1, device_id={"row": peer}, device_id_type=MESH)

    small[0].wait()
    small[1].wait()
    degrees = degree[...].astype(jnp.float32)

    def gather(step, half, at, length):
        rows_at = pl.ds(at, length)
        return [
            send(
                xs.at[step, col, rows_at], xs.at[step, col, rows_at],
                xs_send.at[step, half, d - 1], xs_recv.at[step, half, d - 1],
                {"col": lax.rem(col + d, cols)},
            )
            for d in range(1, cols)
        ]

    xs[0, col] = (prior[...] / degrees).astype(jnp.bfloat16)
    for copy in small[2:]:
        copy.wait()
    for q in range(PARTS):
        sums[q][none] = jnp.zeros((part, edge), jnp.float32)

    def add_tile(s, carry):
        last_out, last_in = carry[0], carry[1:]
        o = outs[0, 0, s]
        i = ins[0, 0, s]
        same = o == last_out
        last_in = [jnp.where(same, h, none) for h in last_in]
        prev = last_in[0]
        for k in range(1, cols):
            prev = jnp.where(i == k, last_in[k], prev)
        for q in range(PARTS):
            tile = buf[s, q * part:(q + 1) * part, :].astype(jnp.float32)
            sums[q][s] = sums[q][prev] + tile
        last_in = [jnp.where(i == k, s, last_in[k]) for k in range(cols)]
        for k in range(0, cols, 2):
            heads[k // 2, s] = last_in[k] + last_in[k + 1] * 65536
        return (o, *last_in)

    carry = (jnp.int32(-1),) + (jnp.int32(none),) * cols
    for g in range(chunks):
        if g == X_CHUNK:
            @pl.when(core == 0)
            def _():
                pl.semaphore_wait(barrier, 2 * (cols - 1) + 1)
                pl.semaphore_signal(x_ready, inc=1, device_id={"row": partner}, device_id_type=MESH)

            @pl.when(core == 1)
            def _():
                pl.semaphore_wait(x_ready, 1)

            first_copies = gather(0, 0, 0, sets)
        if g == Z_CHUNK:
            @pl.when(core == 1)
            def _():
                pl.semaphore_wait(barrier, 2 * (ring - 1) + 1)
                pl.semaphore_signal(z_ready, inc=1, device_id={"row": partner}, device_id_type=MESH)
        tile_copy(g).wait()
        if g + FLIGHT < chunks:
            tile_copy(g + FLIGHT).start()
        carry = lax.fori_loop(g * group, (g + 1) * group, add_tile, carry, unroll=4)

    used = count[0, 0]
    steps = [1 << b for b in reversed(range(slots.bit_length()))]

    def last_slots(o):
        end = jnp.int32(0)
        for step in steps:
            mid = end + step
            inside = mid <= used
            fits = outs[0, 0, jnp.minimum(mid, slots) - 1] <= o
            end = jnp.where(inside & fits, mid, end)
        at = jnp.maximum(end - 1, 0)
        hit = (end > 0) & (outs[0, 0, at] == o)
        found = []
        for k in range(0, cols, 2):
            pair = heads[k // 2, at]
            found.append(jnp.where(hit, pair % 65536, none))
            found.append(jnp.where(hit, pair // 65536, none))
        return found

    def target(n):
        return lax.rem(chip + order[n], ring)

    def build(n):
        for half in range(2):
            places = last_slots(target(n) * 2 + half)
            for k in range(cols):
                for q in range(PARTS):
                    value = sums[q][places[k]]
                    high = value.astype(jnp.bfloat16)
                    low = (value - high.astype(jnp.float32)).astype(jnp.bfloat16)
                    at = k * edge + q * part
                    w[n, at:at + part, half * edge:(half + 1) * edge] = high
                    w[n, depth + at:depth + at + part, half * edge:(half + 1) * edge] = low

    def multiply(x, n, step, half, at):
        both = jnp.dot(x, w[n], preferred_element_type=jnp.float32)
        left, right = both[:, :edge], both[:, edge:]
        rows_at = pl.ds(at, x.shape[0])
        psend[step, n, rows_at] = jnp.where(core == 0, right, left).astype(jnp.bfloat16)
        own[n, rows_at] = jnp.where(core == 0, left, right)
        if step == 0 and n + 1 < ring:
            build(n + 1)
        return send(
            psend.at[step, n, rows_at], precv.at[step, n, rows_at],
            ps_send.at[step, half, n], ps_recv.at[step, half, n], {"row": partner},
        )

    def add_partner(copy, n, step, at, length):
        copy.wait_recv()
        rows_at = pl.ds(at, length)
        total = own[n, rows_at] + precv[step, n, rows_at].astype(jnp.float32)
        if order[n] == 0:
            own[n, rows_at] = total
        else:
            zsend[step, n, rows_at] = total.astype(jnp.bfloat16)

    def send_chip(n, step, half):
        if order[n] == 0:
            return None
        rows_at = pl.ds(half * size, size)
        return send(
            zsend.at[step, n, rows_at], zrecv.at[step, n, rows_at],
            zs_send.at[step, half, n], zs_recv.at[step, half, n], {"row": target(n) * 2 + core},
        )

    def collect(copies, step, half):
        rows_at = pl.ds(half * size, size)
        total = own[ring - 1, rows_at]
        for n in reversed(range(ring - 1)):
            copies[n].wait_recv()
            total += zrecv[step, n, rows_at].astype(jnp.float32)
        return total

    def input_rows(step, at, length):
        parts = [xs[step, k, at:at + length] for k in range(cols)]
        return jnp.concatenate(parts + parts, axis=1)

    build(0)
    for copy in first_copies:
        copy.wait_recv()
    x = input_rows(0, 0, sets)
    pending = []
    chip_copies = [[None] * ring for _ in range(HALVES)]

    @pl.when(core == 0)
    def _():
        pl.semaphore_wait(z_ready, 1)

    def pass_on(step, halves, at, length):
        copy, n = pending.pop(0)
        add_partner(copy, n, step, at, length)
        chip_copies[halves][n] = send_chip(n, step, halves)

    for n in range(ring):
        pending.append((multiply(x, n, 0, 0, 0), n))
        if n >= LAG_FIRST:
            pass_on(0, 0, 0, sets)
    while pending:
        pass_on(0, 0, 0, sets)
    for half in range(1, HALVES):
        for n in range(ring):
            chip_copies[half][n] = send_chip(n, 0, half)

    local_ids = seeds[...].T - (row * cols + col) * edge
    places = lax.broadcasted_iota(jnp.int32, (sets, edge), 1)
    restart = jnp.zeros((sets, edge), jnp.float32)
    for j in range(local_ids.shape[1]):
        restart += (local_ids[:, j:j + 1] == places).astype(jnp.float32)
    prior[...] = (1.0 - damping) * restart

    col_copies = []
    for half in range(HALVES):
        rows_at = pl.ds(half * size, size)
        risk = prior[rows_at] + damping * collect(chip_copies[half], 0, half)
        xs[1, col, rows_at] = (risk / degrees).astype(jnp.bfloat16)
        col_copies.append(gather(1, half, half * size, size))

    chip_copies = [[None] * ring for _ in range(HALVES)]
    for half in range(HALVES):
        for copy in col_copies[half]:
            copy.wait_recv()
        x = input_rows(1, half * size, size)
        for n in range(ring):
            pending.append((multiply(x, n, 1, half, half * size), n))
            if n >= LAG_LAST:
                pass_on(1, half, half * size, size)
        while pending:
            pass_on(1, half, half * size, size)
    for half in range(HALVES):
        rows_at = pl.ds(half * size, size)
        risk_out[rows_at] = prior[rows_at] + damping * collect(chip_copies[half], 1, half)
    for copy in sent:
        copy.wait_send()


def local(tiles, tile_out, tile_in, tile_count, out_degree, seed_ids, prior):
    rows, cols = lax.axis_size("row"), lax.axis_size("col")
    slots, edge = tiles.shape[2], tiles.shape[4]
    sets = prior.shape[0]
    ring = rows // 2
    chunks = math.gcd(slots, CHUNKS)
    vmem = pl.BlockSpec(memory_space=pltpu.VMEM)
    hbm = pl.BlockSpec(memory_space=pltpu.HBM)
    block = (sets, edge)
    dma = pltpu.SemaphoreType.DMA
    return pl.pallas_call(
        functools.partial(kernel, rows, cols, chunks),
        out_shape=jax.ShapeDtypeStruct(block, jnp.float32),
        in_specs=[pl.BlockSpec(memory_space=pltpu.SMEM)] + [hbm] * 6,
        out_specs=vmem,
        scratch_shapes=[
            pltpu.SMEM(tile_out.shape, jnp.int32),
            pltpu.SMEM(tile_in.shape, jnp.int32),
            pltpu.VMEM((1, edge), jnp.int32),
            pltpu.VMEM(seed_ids.shape[::-1], jnp.int32),
            pltpu.VMEM(block, jnp.float32),
            pltpu.VMEM((slots, edge, edge), jnp.bfloat16),
            *[pltpu.VMEM((slots + 1, edge // PARTS, edge), jnp.float32) for _ in range(PARTS)],
            pltpu.SMEM((cols // 2, slots), jnp.int32),
            pltpu.VMEM((ring, 2 * cols * edge, 2 * edge), jnp.bfloat16),
            pltpu.VMEM((ITERATIONS, cols, *block), jnp.bfloat16),
            pltpu.VMEM((ring, *block), jnp.float32),
            pltpu.VMEM((ITERATIONS, ring, *block), jnp.bfloat16),
            pltpu.VMEM((ITERATIONS, ring, *block), jnp.bfloat16),
            pltpu.VMEM((ITERATIONS, ring, *block), jnp.bfloat16),
            pltpu.VMEM((ITERATIONS, ring, *block), jnp.bfloat16),
            dma((5,)),
            dma((chunks,)),
            dma((ITERATIONS, HALVES, cols)),
            dma((ITERATIONS, HALVES, cols)),
            dma((ITERATIONS, HALVES, ring)),
            dma((ITERATIONS, HALVES, ring)),
            dma((ITERATIONS, HALVES, ring)),
            dma((ITERATIONS, HALVES, ring)),
            pltpu.SemaphoreType.REGULAR,
            pltpu.SemaphoreType.REGULAR,
        ],
        compiler_params=pltpu.CompilerParams(
            collective_id=0, has_side_effects=True, vmem_limit_bytes=52 * 1024 * 1024
        ),
    )(
        tile_count,
        *[pltpu.with_memory_space_constraint(a, pltpu.HBM) for a in (
            tile_out,
            tile_in,
            tiles.reshape(slots, edge, edge),
            out_degree.reshape(1, edge),
            seed_ids.T,
            prior,
        )]
    )


def solution(mesh):
    placed = (
        P("row", "col", None, None, None),
        P("row", "col", None),
        P("row", "col", None),
        P("row", "col"),
        P(("row", "col")),
        P("seed", None),
        P("seed", ("row", "col")),
    )
    return jax.shard_map(
        local, mesh=mesh, in_specs=placed, out_specs=P("seed", ("row", "col")), check_vma=False
    )
```

```python
import functools
import math

import jax
import jax.numpy as jnp
from jax import lax
from jax.experimental import pallas as pl
from jax.experimental.pallas import tpu as pltpu
from jax.sharding import PartitionSpec as P

ITERATIONS = 2
PARTS = 4
CHUNKS = 16
FLIGHT = 4
PIECES = (8, 8)
X_CHUNK = 2
Z_CHUNK = 12
LAG_FIRST = 3
damping = 0.85
MESH = pl.DeviceIdType.MESH


def ring_order(ring):
    return sorted(range(ring), key=lambda d: -min(d, ring - d))


def kernel(
    rows, cols, chunks,
    count, outs_in, ins_in, tiles, degree_in, seeds_in, prior_in, risk_out,
    outs, ins, degree, seeds, prior, buf, sum0, sum1, sum2, sum3, heads,
    w, w_other, xs, xs_last, own, psend, precv, zsend, zrecv,
    isem, tsem, ws_send, ws_recv, xs_send, xs_recv, xl_send, xl_recv, ps_send, ps_recv, zs_send, zs_recv,
    x_ready, z_ready,
):
    sums = (sum0, sum1, sum2, sum3)
    slots, edge, _ = buf.shape
    sets = prior.shape[0]
    pieces = []
    for share in PIECES:
        size = sets * share // sum(PIECES)
        pieces.append((pieces[-1][0] + pieces[-1][1] if pieces else 0, size))
    group = slots // chunks
    part = edge // PARTS
    ring = rows // 2
    row = lax.axis_index("row")
    col = lax.axis_index("col")
    core = lax.rem(row, 2)
    chip = row // 2
    partner = row + 1 - 2 * core
    depth = cols * edge
    order = ring_order(ring)
    none = slots
    sent = []

    def tile_copy(g):
        at = pl.ds(g * group, group)
        return pltpu.make_async_copy(tiles.at[at], buf.at[at], tsem.at[g])

    def send(source, target, send_sem, recv_sem, device):
        copy = pltpu.make_async_remote_copy(
            src_ref=source, dst_ref=target, send_sem=send_sem, recv_sem=recv_sem,
            device_id=device, device_id_type=MESH,
        )
        copy.start()
        sent.append(copy)
        return copy

    small = [
        pltpu.make_async_copy(source, place, isem.at[n])
        for n, (source, place) in enumerate((
            (degree_in, degree), (prior_in, prior), (outs_in, outs), (ins_in, ins), (seeds_in, seeds),
        ))
    ]
    for copy in small:
        copy.start()
    for g in range(FLIGHT):
        tile_copy(g).start()

    barrier = pltpu.get_barrier_semaphore()
    for d in range(1, cols):
        pl.semaphore_signal(
            barrier, inc=1, device_id={"row": chip * 2, "col": lax.rem(col + d, cols)}, device_id_type=MESH
        )
    pl.semaphore_signal(barrier, inc=1, device_id={"row": partner}, device_id_type=MESH)
    for d in range(1, ring):
        peer = lax.rem(chip + d, ring) * 2 + 1
        pl.semaphore_signal(barrier, inc=1, device_id={"row": peer}, device_id_type=MESH)

    small[0].wait()
    small[1].wait()
    degrees = degree[...].astype(jnp.float32)

    def gather_first():
        return [
            send(
                xs.at[col], xs.at[col], xs_send.at[d - 1], xs_recv.at[d - 1],
                {"col": lax.rem(col + d, cols)},
            )
            for d in range(1, cols)
        ]

    def gather_last(piece):
        at, size = pieces[piece]
        mine = xs_last.at[core, col, pl.ds(at, size)]
        return [
            send(
                mine, mine, xl_send.at[piece, other, d], xl_recv.at[piece, other, d],
                {"row": row if other == 0 else partner, "col": lax.rem(col + d, cols)},
            )
            for d in ring_order(cols) for other in range(2) if d + other > 0
        ]

    xs[col] = (prior[...] / degrees).astype(jnp.bfloat16)
    for copy in small[2:]:
        copy.wait()
    for q in range(PARTS):
        sums[q][none] = jnp.zeros((part, edge), jnp.float32)

    def add_tile(s, carry):
        last_out, last_in = carry[0], carry[1:]
        o = outs[0, 0, s]
        i = ins[0, 0, s]
        same = o == last_out
        last_in = [jnp.where(same, h, none) for h in last_in]
        prev = last_in[0]
        for k in range(1, cols):
            prev = jnp.where(i == k, last_in[k], prev)
        for q in range(PARTS):
            tile = buf[s, q * part:(q + 1) * part, :].astype(jnp.float32)
            sums[q][s] = sums[q][prev] + tile
        last_in = [jnp.where(i == k, s, last_in[k]) for k in range(cols)]
        for k in range(0, cols, 2):
            heads[k // 2, s] = last_in[k] + last_in[k + 1] * 65536
        return (o, *last_in)

    carry = (jnp.int32(-1),) + (jnp.int32(none),) * cols
    for g in range(chunks):
        if g == X_CHUNK:
            @pl.when(core == 0)
            def _():
                pl.semaphore_wait(barrier, 2 * (cols - 1) + 1)
                pl.semaphore_signal(x_ready, inc=1, device_id={"row": partner}, device_id_type=MESH)

            @pl.when(core == 1)
            def _():
                pl.semaphore_wait(x_ready, 1)

            first_copies = gather_first()
        if g == Z_CHUNK:
            @pl.when(core == 1)
            def _():
                pl.semaphore_wait(barrier, 2 * (ring - 1) + 1)
                pl.semaphore_signal(z_ready, inc=1, device_id={"row": partner}, device_id_type=MESH)
        tile_copy(g).wait()
        if g + FLIGHT < chunks:
            tile_copy(g + FLIGHT).start()
        carry = lax.fori_loop(g * group, (g + 1) * group, add_tile, carry, unroll=4)

    used = count[0, 0]
    steps = [1 << b for b in reversed(range(slots.bit_length()))]

    def last_slots(o):
        end = jnp.int32(0)
        for step in steps:
            mid = end + step
            inside = mid <= used
            fits = outs[0, 0, jnp.minimum(mid, slots) - 1] <= o
            end = jnp.where(inside & fits, mid, end)
        at = jnp.maximum(end - 1, 0)
        hit = (end > 0) & (outs[0, 0, at] == o)
        found = []
        for k in range(0, cols, 2):
            pair = heads[k // 2, at]
            found.append(jnp.where(hit, pair % 65536, none))
            found.append(jnp.where(hit, pair // 65536, none))
        return found

    def target(n):
        return lax.rem(chip + order[n], ring)

    def build(n):
        for half in range(2):
            places = last_slots(target(n) * 2 + half)
            for k in range(cols):
                for q in range(PARTS):
                    value = sums[q][places[k]]
                    high = value.astype(jnp.bfloat16)
                    low = (value - high.astype(jnp.float32)).astype(jnp.bfloat16)
                    at = k * edge + q * part
                    w[n, half, at:at + part] = high
                    w[n, half, depth + at:depth + at + part] = low

    def add_partner(copy, n):
        copy.wait_recv()
        total = own[n] + precv[n].astype(jnp.float32)
        if order[n] == 0:
            own[n] = total
        else:
            zsend[0, n] = total.astype(jnp.bfloat16)

    def send_chip(n, step, piece):
        if order[n] == 0:
            return None
        at, size = pieces[piece]
        rows_at = pl.ds(at, size)
        return send(
            zsend.at[step, n, rows_at], zrecv.at[step, n, rows_at],
            zs_send.at[step, piece, n], zs_recv.at[step, piece, n], {"row": target(n) * 2 + core},
        )

    def collect(copies, step, piece):
        at, size = pieces[piece]
        rows_at = pl.ds(at, size)
        total = own[ring - 1, rows_at]
        for n in reversed(range(ring - 1)):
            copies[n].wait_recv()
            total += zrecv[step, n, rows_at].astype(jnp.float32)
        return total

    build(0)
    for copy in first_copies:
        copy.wait_recv()
    parts = [xs[k] for k in range(cols)]
    x = jnp.concatenate(parts + parts, axis=1)
    chip_copies = [[None] * ring for _ in pieces]

    @pl.when(core == 0)
    def _():
        pl.semaphore_wait(z_ready, 1)

    pending = []

    def pass_on():
        copy, n = pending.pop(0)
        add_partner(copy, n)
        chip_copies[0][n] = send_chip(n, 0, 0)

    for n in range(ring):
        both = jnp.dot(x, jnp.concatenate([w[n, 0], w[n, 1]], axis=1), preferred_element_type=jnp.float32)
        left, right = both[:, :edge], both[:, edge:]
        psend[n] = jnp.where(core == 0, right, left).astype(jnp.bfloat16)
        own[n] = jnp.where(core == 0, left, right)
        if n + 1 < ring:
            build(n + 1)
        pending.append((send(psend.at[n], precv.at[n], ps_send.at[n], ps_recv.at[n], {"row": partner}), n))
        if n >= LAG_FIRST:
            pass_on()
    while pending:
        pass_on()
    for piece in range(1, len(pieces)):
        for n in range(ring):
            chip_copies[piece][n] = send_chip(n, 0, piece)
    w_copies = [
        send(w.at[n, 1 - core], w_other.at[n], ws_send.at[n], ws_recv.at[n], {"row": partner})
        for n in range(ring)
    ]

    local_ids = seeds[...].T - (row * cols + col) * edge
    places = lax.broadcasted_iota(jnp.int32, (sets, edge), 1)
    restart = jnp.zeros((sets, edge), jnp.float32)
    for j in range(local_ids.shape[1]):
        restart += (local_ids[:, j:j + 1] == places).astype(jnp.float32)
    prior[...] = (1.0 - damping) * restart

    col_copies = []
    for piece, (at, size) in enumerate(pieces):
        rows_at = pl.ds(at, size)
        risk = prior[rows_at] + damping * collect(chip_copies[piece], 0, piece)
        xs_last[core, col, rows_at] = (risk / degrees).astype(jnp.bfloat16)
        col_copies.append(gather_last(piece))

    last_copies = [[None] * ring for _ in pieces]

    def store(piece):
        at, size = pieces[piece]
        rows_at = pl.ds(at, size)
        risk_out[rows_at] = prior[rows_at] + damping * collect(last_copies[piece], 1, piece)

    for copy in w_copies:
        copy.wait_recv()
    for piece, (at, size) in enumerate(pieces):
        rows_at = pl.ds(at, size)
        for copy in col_copies[piece]:
            copy.wait_recv()
        near = [xs_last[core, k, rows_at] for k in range(cols)]
        far = [xs_last[1 - core, k, rows_at] for k in range(cols)]
        near = jnp.concatenate(near + near, axis=1)
        far = jnp.concatenate(far + far, axis=1)
        for n in range(0, ring, 2):
            both = jnp.dot(
                near, jnp.concatenate([w[n, core], w[n + 1, core]], axis=1), preferred_element_type=jnp.float32
            ) + jnp.dot(
                far, jnp.concatenate([w_other[n], w_other[n + 1]], axis=1), preferred_element_type=jnp.float32
            )
            for m, total in ((n, both[:, :edge]), (n + 1, both[:, edge:])):
                if order[m] == 0:
                    own[m, rows_at] = total
                else:
                    zsend[1, m, rows_at] = total.astype(jnp.bfloat16)
            for m in (n, n + 1):
                last_copies[piece][m] = send_chip(m, 1, piece)
    for piece in range(len(pieces)):
        store(piece)
    for copy in sent:
        copy.wait_send()


def local(tiles, tile_out, tile_in, tile_count, out_degree, seed_ids, prior):
    rows, cols = lax.axis_size("row"), lax.axis_size("col")
    slots, edge = tiles.shape[2], tiles.shape[4]
    sets = prior.shape[0]
    ring = rows // 2
    chunks = math.gcd(slots, CHUNKS)
    vmem = pl.BlockSpec(memory_space=pltpu.VMEM)
    hbm = pl.BlockSpec(memory_space=pltpu.HBM)
    block = (sets, edge)
    dma = pltpu.SemaphoreType.DMA
    return pl.pallas_call(
        functools.partial(kernel, rows, cols, chunks),
        out_shape=jax.ShapeDtypeStruct(block, jnp.float32),
        in_specs=[pl.BlockSpec(memory_space=pltpu.SMEM)] + [hbm] * 6,
        out_specs=vmem,
        scratch_shapes=[
            pltpu.SMEM(tile_out.shape, jnp.int32),
            pltpu.SMEM(tile_in.shape, jnp.int32),
            pltpu.VMEM((1, edge), jnp.int32),
            pltpu.VMEM(seed_ids.shape[::-1], jnp.int32),
            pltpu.VMEM(block, jnp.float32),
            pltpu.VMEM((slots, edge, edge), jnp.bfloat16),
            *[pltpu.VMEM((slots + 1, edge // PARTS, edge), jnp.float32) for _ in range(PARTS)],
            pltpu.SMEM((cols // 2, slots), jnp.int32),
            pltpu.VMEM((ring, 2, 2 * cols * edge, edge), jnp.bfloat16),
            pltpu.VMEM((ring, 2 * cols * edge, edge), jnp.bfloat16),
            pltpu.VMEM((cols, *block), jnp.bfloat16),
            pltpu.VMEM((2, cols, *block), jnp.bfloat16),
            pltpu.VMEM((ring, *block), jnp.float32),
            pltpu.VMEM((ring, *block), jnp.bfloat16),
            pltpu.VMEM((ring, *block), jnp.bfloat16),
            pltpu.VMEM((ITERATIONS, ring, *block), jnp.bfloat16),
            pltpu.VMEM((ITERATIONS, ring, *block), jnp.bfloat16),
            dma((5,)),
            dma((chunks,)),
            dma((ring,)),
            dma((ring,)),
            dma((cols,)),
            dma((cols,)),
            dma((len(PIECES), 2, cols)),
            dma((len(PIECES), 2, cols)),
            dma((ring,)),
            dma((ring,)),
            dma((ITERATIONS, len(PIECES), ring)),
            dma((ITERATIONS, len(PIECES), ring)),
            pltpu.SemaphoreType.REGULAR,
            pltpu.SemaphoreType.REGULAR,
        ],
        compiler_params=pltpu.CompilerParams(
            collective_id=0, has_side_effects=True, vmem_limit_bytes=52 * 1024 * 1024
        ),
    )(
        tile_count,
        *[pltpu.with_memory_space_constraint(a, pltpu.HBM) for a in (
            tile_out,
            tile_in,
            tiles.reshape(slots, edge, edge),
            out_degree.reshape(1, edge),
            seed_ids.T,
            prior,
        )]
    )


def solution(mesh):
    placed = (
        P("row", "col", None, None, None),
        P("row", "col", None),
        P("row", "col", None),
        P("row", "col"),
        P(("row", "col")),
        P("seed", None),
        P("seed", ("row", "col")),
    )
    return jax.shard_map(
        local, mesh=mesh, in_specs=placed, out_specs=P("seed", ("row", "col")), check_vma=False
    )
```

```python
import functools
import math

import jax
import jax.numpy as jnp
from jax import lax
from jax.experimental import pallas as pl
from jax.experimental.pallas import tpu as pltpu
from jax.sharding import PartitionSpec as P

ITERATIONS = 2
PARTS = 4
CHUNKS = 16
FLIGHT = 4
PIECES = (8, 8)
X_CHUNK = 2
Z_CHUNK = 12
LAG_FIRST = 2
damping = 0.85
MESH = pl.DeviceIdType.MESH


def ring_order(ring):
    return sorted(range(ring), key=lambda d: -min(d, ring - d))


def kernel(
    rows, cols, chunks,
    count, outs_in, ins_in, tiles, degree_in, seeds_in, prior_in, risk_out,
    outs, ins, degree, seeds, prior, buf, sum0, sum1, sum2, sum3, heads,
    w, w_other, xs, xs_last, own, psend, precv, zsend, zrecv,
    isem, tsem, ws_send, ws_recv, xs_send, xs_recv, xl_send, xl_recv, ps_send, ps_recv, zs_send, zs_recv,
    x_ready, z_ready,
):
    sums = (sum0, sum1, sum2, sum3)
    slots, edge, _ = buf.shape
    sets = prior.shape[0]
    pieces = []
    for share in PIECES:
        size = sets * share // sum(PIECES)
        pieces.append((pieces[-1][0] + pieces[-1][1] if pieces else 0, size))
    group = slots // chunks
    part = edge // PARTS
    ring = rows // 2
    row = lax.axis_index("row")
    col = lax.axis_index("col")
    core = lax.rem(row, 2)
    chip = row // 2
    partner = row + 1 - 2 * core
    depth = cols * edge
    order = ring_order(ring)
    none = slots
    sent = []

    def tile_copy(g):
        at = pl.ds(g * group, group)
        return pltpu.make_async_copy(tiles.at[at], buf.at[at], tsem.at[g])

    def send(source, target, send_sem, recv_sem, device):
        copy = pltpu.make_async_remote_copy(
            src_ref=source, dst_ref=target, send_sem=send_sem, recv_sem=recv_sem,
            device_id=device, device_id_type=MESH,
        )
        copy.start()
        sent.append(copy)
        return copy

    small = [
        pltpu.make_async_copy(source, place, isem.at[n])
        for n, (source, place) in enumerate((
            (degree_in, degree), (prior_in, prior), (outs_in, outs), (ins_in, ins), (seeds_in, seeds),
        ))
    ]
    for copy in small:
        copy.start()
    for g in range(FLIGHT):
        tile_copy(g).start()

    barrier = pltpu.get_barrier_semaphore()
    for d in range(1, cols):
        pl.semaphore_signal(
            barrier, inc=1, device_id={"row": chip * 2, "col": lax.rem(col + d, cols)}, device_id_type=MESH
        )
    pl.semaphore_signal(barrier, inc=1, device_id={"row": partner}, device_id_type=MESH)
    for d in range(1, ring):
        peer = lax.rem(chip + d, ring) * 2 + 1
        pl.semaphore_signal(barrier, inc=1, device_id={"row": peer}, device_id_type=MESH)

    small[0].wait()
    small[1].wait()
    degrees = degree[...].astype(jnp.float32)

    def gather_first():
        return [
            send(
                xs.at[col], xs.at[col], xs_send.at[d - 1], xs_recv.at[d - 1],
                {"col": lax.rem(col + d, cols)},
            )
            for d in range(1, cols)
        ]

    def gather_last(piece):
        at, size = pieces[piece]
        mine = xs_last.at[core, col, pl.ds(at, size)]
        return [
            send(
                mine, mine, xl_send.at[piece, other, d], xl_recv.at[piece, other, d],
                {"row": row if other == 0 else partner, "col": lax.rem(col + d, cols)},
            )
            for d in ring_order(cols) for other in range(2) if d + other > 0
        ]

    xs[col] = (prior[...] / degrees).astype(jnp.bfloat16)
    for copy in small[2:]:
        copy.wait()
    for q in range(PARTS):
        sums[q][none] = jnp.zeros((part, edge), jnp.float32)

    def add_tile(s, carry):
        last_out, last_in = carry[0], carry[1:]
        o = outs[0, 0, s]
        i = ins[0, 0, s]
        same = o == last_out
        last_in = [jnp.where(same, h, none) for h in last_in]
        prev = last_in[0]
        for k in range(1, cols):
            prev = jnp.where(i == k, last_in[k], prev)
        for q in range(PARTS):
            tile = buf[s, q * part:(q + 1) * part, :].astype(jnp.float32)
            sums[q][s] = sums[q][prev] + tile
        last_in = [jnp.where(i == k, s, last_in[k]) for k in range(cols)]
        for k in range(0, cols, 2):
            heads[k // 2, s] = last_in[k] + last_in[k + 1] * 65536
        return (o, *last_in)

    carry = (jnp.int32(-1),) + (jnp.int32(none),) * cols
    for g in range(chunks):
        if g == X_CHUNK:
            @pl.when(core == 0)
            def _():
                pl.semaphore_wait(barrier, 2 * (cols - 1) + 1)
                pl.semaphore_signal(x_ready, inc=1, device_id={"row": partner}, device_id_type=MESH)

            @pl.when(core == 1)
            def _():
                pl.semaphore_wait(x_ready, 1)

            first_copies = gather_first()
        if g == Z_CHUNK:
            @pl.when(core == 1)
            def _():
                pl.semaphore_wait(barrier, 2 * (ring - 1) + 1)
                pl.semaphore_signal(z_ready, inc=1, device_id={"row": partner}, device_id_type=MESH)
        tile_copy(g).wait()
        if g + FLIGHT < chunks:
            tile_copy(g + FLIGHT).start()
        carry = lax.fori_loop(g * group, (g + 1) * group, add_tile, carry, unroll=4)

    used = count[0, 0]
    steps = [1 << b for b in reversed(range(slots.bit_length()))]

    def last_slots(o):
        end = jnp.int32(0)
        for step in steps:
            mid = end + step
            inside = mid <= used
            fits = outs[0, 0, jnp.minimum(mid, slots) - 1] <= o
            end = jnp.where(inside & fits, mid, end)
        at = jnp.maximum(end - 1, 0)
        hit = (end > 0) & (outs[0, 0, at] == o)
        found = []
        for k in range(0, cols, 2):
            pair = heads[k // 2, at]
            found.append(jnp.where(hit, pair % 65536, none))
            found.append(jnp.where(hit, pair // 65536, none))
        return found

    def target(n):
        return lax.rem(chip + order[n], ring)

    def build(n):
        for half in range(2):
            places = last_slots(target(n) * 2 + half)
            for k in range(cols):
                for q in range(PARTS):
                    value = sums[q][places[k]]
                    high = value.astype(jnp.bfloat16)
                    low = (value - high.astype(jnp.float32)).astype(jnp.bfloat16)
                    at = k * edge + q * part
                    w[n, half, at:at + part] = high
                    w[n, half, depth + at:depth + at + part] = low

    def add_partner(copy, n):
        copy.wait_recv()
        total = own[n] + precv[n].astype(jnp.float32)
        if order[n] == 0:
            own[n] = total
        else:
            zsend[0, n] = total.astype(jnp.bfloat16)

    def send_chip(n, step, piece):
        if order[n] == 0:
            return None
        at, size = pieces[piece]
        rows_at = pl.ds(at, size)
        return send(
            zsend.at[step, n, rows_at], zrecv.at[step, n, rows_at],
            zs_send.at[step, piece, n], zs_recv.at[step, piece, n], {"row": target(n) * 2 + core},
        )

    def collect(copies, step, piece):
        at, size = pieces[piece]
        rows_at = pl.ds(at, size)
        total = own[ring - 1, rows_at]
        for n in reversed(range(ring - 1)):
            copies[n].wait_recv()
            total += zrecv[step, n, rows_at].astype(jnp.float32)
        return total

    build(0)
    for copy in first_copies:
        copy.wait_recv()
    parts = [xs[k] for k in range(cols)]
    x = jnp.concatenate(parts + parts, axis=1)
    chip_copies = [[None] * ring for _ in pieces]

    @pl.when(core == 0)
    def _():
        pl.semaphore_wait(z_ready, 1)

    pending = []

    def pass_on():
        copy, n = pending.pop(0)
        add_partner(copy, n)
        chip_copies[0][n] = send_chip(n, 0, 0)

    for n in range(ring):
        both = jnp.dot(x, jnp.concatenate([w[n, 0], w[n, 1]], axis=1), preferred_element_type=jnp.float32)
        left, right = both[:, :edge], both[:, edge:]
        psend[n] = jnp.where(core == 0, right, left).astype(jnp.bfloat16)
        own[n] = jnp.where(core == 0, left, right)
        if n + 1 < ring:
            build(n + 1)
        pending.append((send(psend.at[n], precv.at[n], ps_send.at[n], ps_recv.at[n], {"row": partner}), n))
        if n >= LAG_FIRST:
            pass_on()
    while pending:
        pass_on()
    for piece in range(1, len(pieces)):
        for n in range(ring):
            chip_copies[piece][n] = send_chip(n, 0, piece)
    w_copies = [
        send(w.at[n, 1 - core, pl.ds(0, depth)], w_other.at[n], ws_send.at[n], ws_recv.at[n], {"row": partner})
        for n in range(ring)
    ]

    local_ids = seeds[...].T - (row * cols + col) * edge
    places = lax.broadcasted_iota(jnp.int32, (sets, edge), 1)
    restart = jnp.zeros((sets, edge), jnp.float32)
    for j in range(local_ids.shape[1]):
        restart += (local_ids[:, j:j + 1] == places).astype(jnp.float32)
    prior[...] = (1.0 - damping) * restart

    col_copies = []
    for piece, (at, size) in enumerate(pieces):
        rows_at = pl.ds(at, size)
        risk = prior[rows_at] + damping * collect(chip_copies[piece], 0, piece)
        xs_last[core, col, rows_at] = (risk / degrees).astype(jnp.bfloat16)
        col_copies.append(gather_last(piece))

    last_copies = [[None] * ring for _ in pieces]

    def store(piece):
        at, size = pieces[piece]
        rows_at = pl.ds(at, size)
        risk_out[rows_at] = prior[rows_at] + damping * collect(last_copies[piece], 1, piece)

    for copy in w_copies:
        copy.wait_recv()
    for piece, (at, size) in enumerate(pieces):
        rows_at = pl.ds(at, size)
        for copy in col_copies[piece]:
            copy.wait_recv()
        near = [xs_last[core, k, rows_at] for k in range(cols)]
        far = [xs_last[1 - core, k, rows_at] for k in range(cols)]
        x = jnp.concatenate(near + far, axis=1)
        for n in range(0, ring, 2):
            mine = jnp.concatenate([w[n, core, :depth], w[n + 1, core, :depth]], axis=1)
            other = jnp.concatenate([w_other[n], w_other[n + 1]], axis=1)
            both = jnp.dot(x, jnp.concatenate([mine, other], axis=0), preferred_element_type=jnp.float32)
            for m, total in ((n, both[:, :edge]), (n + 1, both[:, edge:])):
                if order[m] == 0:
                    own[m, rows_at] = total
                else:
                    zsend[1, m, rows_at] = total.astype(jnp.bfloat16)
            for m in (n, n + 1):
                last_copies[piece][m] = send_chip(m, 1, piece)
    for piece in range(len(pieces)):
        store(piece)
    for copy in sent:
        copy.wait_send()


def local(tiles, tile_out, tile_in, tile_count, out_degree, seed_ids, prior):
    rows, cols = lax.axis_size("row"), lax.axis_size("col")
    slots, edge = tiles.shape[2], tiles.shape[4]
    sets = prior.shape[0]
    ring = rows // 2
    chunks = math.gcd(slots, CHUNKS)
    vmem = pl.BlockSpec(memory_space=pltpu.VMEM)
    hbm = pl.BlockSpec(memory_space=pltpu.HBM)
    block = (sets, edge)
    dma = pltpu.SemaphoreType.DMA
    return pl.pallas_call(
        functools.partial(kernel, rows, cols, chunks),
        out_shape=jax.ShapeDtypeStruct(block, jnp.float32),
        in_specs=[pl.BlockSpec(memory_space=pltpu.SMEM)] + [hbm] * 6,
        out_specs=vmem,
        scratch_shapes=[
            pltpu.SMEM(tile_out.shape, jnp.int32),
            pltpu.SMEM(tile_in.shape, jnp.int32),
            pltpu.VMEM((1, edge), jnp.int32),
            pltpu.VMEM(seed_ids.shape[::-1], jnp.int32),
            pltpu.VMEM(block, jnp.float32),
            pltpu.VMEM((slots, edge, edge), jnp.bfloat16),
            *[pltpu.VMEM((slots + 1, edge // PARTS, edge), jnp.float32) for _ in range(PARTS)],
            pltpu.SMEM((cols // 2, slots), jnp.int32),
            pltpu.VMEM((ring, 2, 2 * cols * edge, edge), jnp.bfloat16),
            pltpu.VMEM((ring, cols * edge, edge), jnp.bfloat16),
            pltpu.VMEM((cols, *block), jnp.bfloat16),
            pltpu.VMEM((2, cols, *block), jnp.bfloat16),
            pltpu.VMEM((ring, *block), jnp.float32),
            pltpu.VMEM((ring, *block), jnp.bfloat16),
            pltpu.VMEM((ring, *block), jnp.bfloat16),
            pltpu.VMEM((ITERATIONS, ring, *block), jnp.bfloat16),
            pltpu.VMEM((ITERATIONS, ring, *block), jnp.bfloat16),
            dma((5,)),
            dma((chunks,)),
            dma((ring,)),
            dma((ring,)),
            dma((cols,)),
            dma((cols,)),
            dma((len(PIECES), 2, cols)),
            dma((len(PIECES), 2, cols)),
            dma((ring,)),
            dma((ring,)),
            dma((ITERATIONS, len(PIECES), ring)),
            dma((ITERATIONS, len(PIECES), ring)),
            pltpu.SemaphoreType.REGULAR,
            pltpu.SemaphoreType.REGULAR,
        ],
        compiler_params=pltpu.CompilerParams(
            collective_id=0, has_side_effects=True, vmem_limit_bytes=52 * 1024 * 1024
        ),
    )(
        tile_count,
        *[pltpu.with_memory_space_constraint(a, pltpu.HBM) for a in (
            tile_out,
            tile_in,
            tiles.reshape(slots, edge, edge),
            out_degree.reshape(1, edge),
            seed_ids.T,
            prior,
        )]
    )


def solution(mesh):
    placed = (
        P("row", "col", None, None, None),
        P("row", "col", None),
        P("row", "col", None),
        P("row", "col"),
        P(("row", "col")),
        P("seed", None),
        P("seed", ("row", "col")),
    )
    return jax.shard_map(
        local, mesh=mesh, in_specs=placed, out_specs=P("seed", ("row", "col")), check_vma=False
    )
```

```python
import functools
import math

import jax
import jax.numpy as jnp
from jax import lax
from jax.experimental import pallas as pl
from jax.experimental.pallas import tpu as pltpu
from jax.sharding import PartitionSpec as P

ITERATIONS = 2
PARTS = 4
CHUNKS = 16
FLIGHT = 4
PIECES = (8, 8)
X_CHUNK = 2
Z_CHUNK = 12
LAG_FIRST = 2
damping = 0.85
MESH = pl.DeviceIdType.MESH


def ring_order(ring):
    return sorted(range(ring), key=lambda d: -min(d, ring - d))


def kernel(
    rows, cols, chunks,
    count, outs_in, ins_in, tiles, degree_in, seeds_in, prior_in, risk_out,
    outs, ins, degree, seeds, prior, buf, sum0, sum1, sum2, sum3, heads,
    w, w_other, xs, xs_last, own, psend, precv, zsend, zrecv,
    isem, tsem, ws_send, ws_recv, xs_send, xs_recv, xl_send, xl_recv, ps_send, ps_recv, zs_send, zs_recv,
    x_ready, z_ready,
):
    sums = (sum0, sum1, sum2, sum3)
    slots, edge, _ = buf.shape
    sets = prior.shape[0]
    pieces = []
    for share in PIECES:
        size = sets * share // sum(PIECES)
        pieces.append((pieces[-1][0] + pieces[-1][1] if pieces else 0, size))
    group = slots // chunks
    part = edge // PARTS
    ring = rows // 2
    row = lax.axis_index("row")
    col = lax.axis_index("col")
    core = lax.rem(row, 2)
    chip = row // 2
    partner = row + 1 - 2 * core
    depth = cols * edge
    order = ring_order(ring)
    none = slots
    sent = []

    def tile_copy(g):
        at = pl.ds(g * group, group)
        return pltpu.make_async_copy(tiles.at[at], buf.at[at], tsem.at[g])

    def send(source, target, send_sem, recv_sem, device):
        copy = pltpu.make_async_remote_copy(
            src_ref=source, dst_ref=target, send_sem=send_sem, recv_sem=recv_sem,
            device_id=device, device_id_type=MESH,
        )
        copy.start()
        sent.append(copy)
        return copy

    small = [
        pltpu.make_async_copy(source, place, isem.at[n])
        for n, (source, place) in enumerate((
            (degree_in, degree), (prior_in, prior), (outs_in, outs), (ins_in, ins), (seeds_in, seeds),
        ))
    ]
    for copy in small:
        copy.start()
    for g in range(FLIGHT):
        tile_copy(g).start()

    barrier = pltpu.get_barrier_semaphore()
    for d in range(1, cols):
        pl.semaphore_signal(
            barrier, inc=1, device_id={"row": chip * 2, "col": lax.rem(col + d, cols)}, device_id_type=MESH
        )
    pl.semaphore_signal(barrier, inc=1, device_id={"row": partner}, device_id_type=MESH)
    for d in range(1, ring):
        peer = lax.rem(chip + d, ring) * 2 + 1
        pl.semaphore_signal(barrier, inc=1, device_id={"row": peer}, device_id_type=MESH)

    small[0].wait()
    small[1].wait()
    degrees = degree[...].astype(jnp.float32)

    def gather_first():
        return [
            send(
                xs.at[col], xs.at[col], xs_send.at[d - 1], xs_recv.at[d - 1],
                {"col": lax.rem(col + d, cols)},
            )
            for d in range(1, cols)
        ]

    def gather_last(piece):
        at, size = pieces[piece]
        mine = xs_last.at[core, col, pl.ds(at, size)]
        return [
            send(
                mine, mine, xl_send.at[piece, other, d], xl_recv.at[piece, other, d],
                {"row": row if other == 0 else partner, "col": lax.rem(col + d, cols)},
            )
            for d in ring_order(cols) for other in range(2) if d + other > 0
        ]

    xs[col] = (prior[...] / degrees).astype(jnp.bfloat16)
    for copy in small[2:]:
        copy.wait()
    for q in range(PARTS):
        sums[q][none] = jnp.zeros((part, edge), jnp.float32)

    def add_tile(s, carry):
        last_out, last_in = carry[0], carry[1:]
        o = outs[0, 0, s]
        i = ins[0, 0, s]
        same = o == last_out
        last_in = [jnp.where(same, h, none) for h in last_in]
        prev = last_in[0]
        for k in range(1, cols):
            prev = jnp.where(i == k, last_in[k], prev)
        for q in range(PARTS):
            tile = buf[s, q * part:(q + 1) * part, :].astype(jnp.float32)
            sums[q][s] = sums[q][prev] + tile
        last_in = [jnp.where(i == k, s, last_in[k]) for k in range(cols)]
        for k in range(0, cols, 2):
            heads[k // 2, s] = last_in[k] + last_in[k + 1] * 65536
        return (o, *last_in)

    carry = (jnp.int32(-1),) + (jnp.int32(none),) * cols
    for g in range(chunks):
        if g == X_CHUNK:
            @pl.when(core == 0)
            def _():
                pl.semaphore_wait(barrier, 2 * (cols - 1) + 1)
                pl.semaphore_signal(x_ready, inc=1, device_id={"row": partner}, device_id_type=MESH)

            @pl.when(core == 1)
            def _():
                pl.semaphore_wait(x_ready, 1)

            first_copies = gather_first()
        if g == Z_CHUNK:
            @pl.when(core == 1)
            def _():
                pl.semaphore_wait(barrier, 2 * (ring - 1) + 1)
                pl.semaphore_signal(z_ready, inc=1, device_id={"row": partner}, device_id_type=MESH)
        tile_copy(g).wait()
        if g + FLIGHT < chunks:
            tile_copy(g + FLIGHT).start()
        carry = lax.fori_loop(g * group, (g + 1) * group, add_tile, carry, unroll=4)

    used = count[0, 0]
    steps = [1 << b for b in reversed(range(slots.bit_length()))]

    def last_slots(o):
        end = jnp.int32(0)
        for step in steps:
            mid = end + step
            inside = mid <= used
            fits = outs[0, 0, jnp.minimum(mid, slots) - 1] <= o
            end = jnp.where(inside & fits, mid, end)
        at = jnp.maximum(end - 1, 0)
        hit = (end > 0) & (outs[0, 0, at] == o)
        found = []
        for k in range(0, cols, 2):
            pair = heads[k // 2, at]
            found.append(jnp.where(hit, pair % 65536, none))
            found.append(jnp.where(hit, pair // 65536, none))
        return found

    def target(n):
        return lax.rem(chip + order[n], ring)

    def build(n):
        for half in range(2):
            places = last_slots(target(n) * 2 + half)
            for k in range(cols):
                for q in range(PARTS):
                    value = sums[q][places[k]]
                    high = value.astype(jnp.bfloat16)
                    low = (value - high.astype(jnp.float32)).astype(jnp.bfloat16)
                    at = k * edge + q * part
                    w[n, half, at:at + part] = high
                    w[n, half, depth + at:depth + at + part] = low

    def add_partner(copy, n):
        copy.wait_recv()
        total = own[n] + precv[n].astype(jnp.float32)
        if order[n] == 0:
            own[n] = total
        else:
            zsend[0, n] = total.astype(jnp.bfloat16)

    def send_chip(n, step, piece):
        if order[n] == 0:
            return None
        at, size = pieces[piece]
        rows_at = pl.ds(at, size)
        return send(
            zsend.at[step, n, rows_at], zrecv.at[step, n, rows_at],
            zs_send.at[step, piece, n], zs_recv.at[step, piece, n], {"row": target(n) * 2 + core},
        )

    def collect(copies, step, piece):
        at, size = pieces[piece]
        rows_at = pl.ds(at, size)
        total = own[ring - 1, rows_at]
        for n in reversed(range(ring - 1)):
            copies[n].wait_recv()
            total += zrecv[step, n, rows_at].astype(jnp.float32)
        return total

    build(0)
    for copy in first_copies:
        copy.wait_recv()
    parts = [xs[k] for k in range(cols)]
    x = jnp.concatenate(parts + parts, axis=1)
    chip_copies = [[None] * ring for _ in pieces]

    @pl.when(core == 0)
    def _():
        pl.semaphore_wait(z_ready, 1)

    pending = []

    def pass_on():
        copy, n = pending.pop(0)
        add_partner(copy, n)
        chip_copies[0][n] = send_chip(n, 0, 0)

    for n in range(ring):
        both = jnp.dot(x, jnp.concatenate([w[n, 0], w[n, 1]], axis=1), preferred_element_type=jnp.float32)
        left, right = both[:, :edge], both[:, edge:]
        psend[n] = jnp.where(core == 0, right, left).astype(jnp.bfloat16)
        own[n] = jnp.where(core == 0, left, right)
        if n + 1 < ring:
            build(n + 1)
        pending.append((send(psend.at[n], precv.at[n], ps_send.at[n], ps_recv.at[n], {"row": partner}), n))
        if n >= LAG_FIRST:
            pass_on()
    while pending:
        pass_on()
    for piece in range(1, len(pieces)):
        for n in range(ring):
            chip_copies[piece][n] = send_chip(n, 0, piece)
    local_ids = seeds[...].T - (row * cols + col) * edge
    places = lax.broadcasted_iota(jnp.int32, (sets, edge), 1)
    restart = jnp.zeros((sets, edge), jnp.float32)
    for j in range(local_ids.shape[1]):
        restart += (local_ids[:, j:j + 1] == places).astype(jnp.float32)
    prior[...] = (1.0 - damping) * restart

    col_copies = []
    for piece, (at, size) in enumerate(pieces):
        rows_at = pl.ds(at, size)
        risk = prior[rows_at] + damping * collect(chip_copies[piece], 0, piece)
        xs_last[core, col, rows_at] = (risk / degrees).astype(jnp.bfloat16)
        col_copies.append(gather_last(piece))
        if piece == 0:
            w_copies = [
                send(w.at[n, 1 - core, pl.ds(0, depth)], w_other.at[n], ws_send.at[n], ws_recv.at[n], {"row": partner})
                for n in range(ring)
            ]

    last_copies = [[None] * ring for _ in pieces]

    def store(piece):
        at, size = pieces[piece]
        rows_at = pl.ds(at, size)
        risk_out[rows_at] = prior[rows_at] + damping * collect(last_copies[piece], 1, piece)

    for copy in w_copies:
        copy.wait_recv()
    for piece, (at, size) in enumerate(pieces):
        rows_at = pl.ds(at, size)
        for copy in col_copies[piece]:
            copy.wait_recv()
        near = [xs_last[core, k, rows_at] for k in range(cols)]
        far = [xs_last[1 - core, k, rows_at] for k in range(cols)]
        x = jnp.concatenate(near + far, axis=1)
        for n in range(0, ring, 2):
            mine = jnp.concatenate([w[n, core, :depth], w[n + 1, core, :depth]], axis=1)
            other = jnp.concatenate([w_other[n], w_other[n + 1]], axis=1)
            both = jnp.dot(x, jnp.concatenate([mine, other], axis=0), preferred_element_type=jnp.float32)
            for m, total in ((n, both[:, :edge]), (n + 1, both[:, edge:])):
                if order[m] == 0:
                    own[m, rows_at] = total
                else:
                    zsend[1, m, rows_at] = total.astype(jnp.bfloat16)
            for m in (n, n + 1):
                last_copies[piece][m] = send_chip(m, 1, piece)
    for piece in range(len(pieces)):
        store(piece)
    for copy in sent:
        copy.wait_send()


def local(tiles, tile_out, tile_in, tile_count, out_degree, seed_ids, prior):
    rows, cols = lax.axis_size("row"), lax.axis_size("col")
    slots, edge = tiles.shape[2], tiles.shape[4]
    sets = prior.shape[0]
    ring = rows // 2
    chunks = math.gcd(slots, CHUNKS)
    vmem = pl.BlockSpec(memory_space=pltpu.VMEM)
    hbm = pl.BlockSpec(memory_space=pltpu.HBM)
    block = (sets, edge)
    dma = pltpu.SemaphoreType.DMA
    return pl.pallas_call(
        functools.partial(kernel, rows, cols, chunks),
        out_shape=jax.ShapeDtypeStruct(block, jnp.float32),
        in_specs=[pl.BlockSpec(memory_space=pltpu.SMEM)] + [hbm] * 6,
        out_specs=vmem,
        scratch_shapes=[
            pltpu.SMEM(tile_out.shape, jnp.int32),
            pltpu.SMEM(tile_in.shape, jnp.int32),
            pltpu.VMEM((1, edge), jnp.int32),
            pltpu.VMEM(seed_ids.shape[::-1], jnp.int32),
            pltpu.VMEM(block, jnp.float32),
            pltpu.VMEM((slots, edge, edge), jnp.bfloat16),
            *[pltpu.VMEM((slots + 1, edge // PARTS, edge), jnp.float32) for _ in range(PARTS)],
            pltpu.SMEM((cols // 2, slots), jnp.int32),
            pltpu.VMEM((ring, 2, 2 * cols * edge, edge), jnp.bfloat16),
            pltpu.VMEM((ring, cols * edge, edge), jnp.bfloat16),
            pltpu.VMEM((cols, *block), jnp.bfloat16),
            pltpu.VMEM((2, cols, *block), jnp.bfloat16),
            pltpu.VMEM((ring, *block), jnp.float32),
            pltpu.VMEM((ring, *block), jnp.bfloat16),
            pltpu.VMEM((ring, *block), jnp.bfloat16),
            pltpu.VMEM((ITERATIONS, ring, *block), jnp.bfloat16),
            pltpu.VMEM((ITERATIONS, ring, *block), jnp.bfloat16),
            dma((5,)),
            dma((chunks,)),
            dma((ring,)),
            dma((ring,)),
            dma((cols,)),
            dma((cols,)),
            dma((len(PIECES), 2, cols)),
            dma((len(PIECES), 2, cols)),
            dma((ring,)),
            dma((ring,)),
            dma((ITERATIONS, len(PIECES), ring)),
            dma((ITERATIONS, len(PIECES), ring)),
            pltpu.SemaphoreType.REGULAR,
            pltpu.SemaphoreType.REGULAR,
        ],
        compiler_params=pltpu.CompilerParams(
            collective_id=0, has_side_effects=True, vmem_limit_bytes=52 * 1024 * 1024
        ),
    )(
        tile_count,
        *[pltpu.with_memory_space_constraint(a, pltpu.HBM) for a in (
            tile_out,
            tile_in,
            tiles.reshape(slots, edge, edge),
            out_degree.reshape(1, edge),
            seed_ids.T,
            prior,
        )]
    )


def solution(mesh):
    placed = (
        P("row", "col", None, None, None),
        P("row", "col", None),
        P("row", "col", None),
        P("row", "col"),
        P(("row", "col")),
        P("seed", None),
        P("seed", ("row", "col")),
    )
    return jax.shard_map(
        local, mesh=mesh, in_specs=placed, out_specs=P("seed", ("row", "col")), check_vma=False
    )
```
